32 devices in a mesh: gx: 16 (over z, x, core), gz: 2 (over y).
Axes of the slice: x: 2, y: 2, z: 4, core: 2. Of those that a mesh axis runs over, the one named last changes fastest.
Arguments:
- overdensity_ratio: float32 [2, 1024, 32, 128], P('gz', 'gx'), may hold values from 0.07 to 15
- thermal_state: float32 [2, 1024, 32, 128], P('gz', 'gx'), may hold values from 0.3 to 3
- residual_drift: float32 [2, 1024, 32, 128], P('gz', 'gx'), may hold values from -0.45 to 0.45
- peculiar_displacement: int32 [2, 1024, 32, 128], P('gz', 'gx'), may hold values from -4 to 4
- doppler_spread: int32 [32], replicated, may hold values from 1 to 4, as said below
Outputs:
- flux: float32 [2, 1024, 32, 128], P('gz', 'gx')
- scale: float32 [32, 128], P('gx')
The draws below stay inside these ranges and needn't reach their ends.
Inputs may be any that keep to these rules, and one draw needn't show every extreme that they name: `doppler_spread`: some column has half width 4.
All inputs are finite; a program needn't handle non-finite values.
Results may differ from the reference program's by a relative error of at most 0.0003.
Values sent between devices are 32-bit elements; how exact they have to be, the bound alone decides.
A program may use at most 64 MiB of HBM per device.

```python
import math
import jax
import jax.numpy as jnp
from jax import lax

SHEET_VOXELS = 128
OMAX = 4
WMAX = 4
ITERS = 8
REACH = 8
PIECE_SPAN = 1024
PIECE_TALLY = 2
SIGHTLINE_TOTAL = 32


def draw_overdensity_ratio(key, part):
    shape = (PIECE_TALLY, PIECE_SPAN, SIGHTLINE_TOTAL, SHEET_VOXELS)
    noise_key = jax.random.fold_in(key, 11)
    segment = lax.broadcasted_iota(jnp.float32, shape, 0)
    within = lax.broadcasted_iota(jnp.float32, shape, 1)
    position = (segment * PIECE_SPAN + within) / (PIECE_TALLY * PIECE_SPAN)
    inner = within / PIECE_SPAN
    base = jnp.exp(jax.random.uniform(noise_key, shape, jnp.float32, -1.6, 1.6))
    trend = jnp.exp(1.2 * (position - 0.5) + 0.8 * (inner - 0.5))
    return base * trend


def draw_doppler_spread(key, part):
    width_key = jax.random.fold_in(key, 21)
    spot_key = jax.random.fold_in(key, 22)
    widths = jax.random.randint(width_key, (SIGHTLINE_TOTAL,), 1, WMAX + 1)
    spot = jax.random.randint(spot_key, (), 0, SIGHTLINE_TOTAL)
    return jnp.where(jnp.arange(SIGHTLINE_TOTAL) == spot, WMAX, widths).astype(jnp.int32)


def place_ends(result, stream_key, least, largest):
    shape = result.shape
    place = [jax.random.randint(jax.random.fold_in(stream_key, axis), (), 0, shape[axis]) for axis in range(len(shape))]
    result = result.at[tuple(place)].set(least)
    longest = shape.index(max(shape))
    place[longest] = (place[longest] + 1) % shape[longest]
    return result.at[tuple(place)].set(largest)


def block_scale(key, dims, cuts, least, high):
    factor_of = 1.0
    for dim, shards_of in cuts:
        heights = jax.random.uniform(jax.random.fold_in(jax.random.fold_in(key, 6), dim), (shards_of,), jnp.float32, least / len(cuts), high / len(cuts))
        factor_of = factor_of * jnp.repeat(jnp.exp(heights), dims[dim] // shards_of).reshape((-1,) + (1,) * (len(dims) - 1 - dim))
    return factor_of


def setup_inputs(seed: int = 0) -> dict:
    streams_of = jax.random.split(jax.random.key(seed), 6)
    return {
        "overdensity_ratio": draw_overdensity_ratio(jax.random.fold_in(streams_of[5], 71), 0),
        "thermal_state": jnp.clip(jnp.exp(math.log(3.0) - 2.3025851 * jax.random.uniform(streams_of[1], (PIECE_TALLY, PIECE_SPAN, SIGHTLINE_TOTAL, SHEET_VOXELS), jnp.float32) ** block_scale(streams_of[1], (PIECE_TALLY, PIECE_SPAN, SIGHTLINE_TOTAL, SHEET_VOXELS), ((0, 2), (1, 16)), -0.2, 0.2)), 0.3, 3.0),
        "residual_drift": jnp.clip(jax.random.uniform(streams_of[2], (PIECE_TALLY, PIECE_SPAN, SIGHTLINE_TOTAL, SHEET_VOXELS), jnp.float32, -0.45, 0.45) * block_scale(streams_of[2], (PIECE_TALLY, PIECE_SPAN, SIGHTLINE_TOTAL, SHEET_VOXELS), ((0, 2), (1, 16)), -0.4, 0.0), -0.45, 0.45),
        "peculiar_displacement": place_ends(jax.random.randint(streams_of[3], (PIECE_TALLY, PIECE_SPAN, SIGHTLINE_TOTAL, SHEET_VOXELS), -OMAX, OMAX + 1), jax.random.fold_in(streams_of[3], 1), -OMAX, OMAX).astype(jnp.int32),
        "doppler_spread": draw_doppler_spread(jax.random.fold_in(streams_of[5], 71), 0),
    }


def prepare_arrays(overdensity_ratio, thermal_state, residual_drift, peculiar_displacement):
    inverted_quantity = 1.0 / (1.2 * jnp.sqrt(thermal_state))
    profile_factor = 0.05 * overdensity_ratio * overdensity_ratio * jnp.exp(-0.7 * jnp.log(thermal_state)) * inverted_quantity / math.sqrt(math.pi)
    central_voxel = peculiar_displacement.astype(jnp.float32) + residual_drift
    return (profile_factor, central_voxel, inverted_quantity)

def column_depth(column):
    profile_factor, central_voxel, inverted_quantity, shifts, width = column
    total = jnp.zeros(profile_factor.shape, jnp.float32)
    for step in range(2 * REACH + 1):
        shift = step - REACH
        gap = jnp.float32(shift) - central_voxel
        keep = jnp.abs(shift - shifts) <= width
        term = jnp.where(keep, profile_factor * jnp.exp(-jnp.square(gap * inverted_quantity)), jnp.float32(0.0))
        total = total + jnp.roll(term, shift, axis=0)
    return total

def reference(overdensity_ratio, thermal_state, residual_drift, peculiar_displacement, doppler_spread):
    shape = overdensity_ratio.shape
    profile_factor, central_voxel, inverted_quantity = prepare_arrays(overdensity_ratio, thermal_state, residual_drift, peculiar_displacement)
    length = shape[0] * shape[1]

    def lines(field):
        return jnp.transpose(field.reshape(length, shape[2], shape[3]), (1, 0, 2))
    tau_lines = lax.map(column_depth, (lines(profile_factor), lines(central_voxel), lines(inverted_quantity), lines(peculiar_displacement), doppler_spread))
    tau = jnp.transpose(tau_lines, (1, 0, 2)).reshape(shape)
    cells = jnp.float32(length)
    level = jnp.zeros((shape[2], shape[3]), jnp.float32)
    for step in range(ITERS):
        factor = jnp.exp(level)
        damped = jnp.exp(-factor[None, None] * tau)
        first = lax.optimization_barrier(jnp.sum(damped, axis=(0, 1)))
        second = lax.optimization_barrier(jnp.sum(tau * damped, axis=(0, 1)))
        level = level - 0.4 * (first / cells - 0.35) / (-factor * second / cells)
    scale = jnp.exp(level)
    return (jnp.exp(-scale[None, None] * tau), scale)
```

```python
import functools
import math

import jax
import jax.numpy as jnp
from jax import lax
from jax.experimental import pallas as pl
from jax.experimental.pallas import tpu as pltpu
from jax.sharding import PartitionSpec as P

ITERS = 8
REACH = 8
BAND = 4
LOG2E = math.log2(math.e)
PEAK = 0.05 / (1.2 * math.sqrt(math.pi))


def spread_terms(overdensity, thermal, drift, masks):
    log_t = jnp.log(thermal)
    q = (LOG2E / 1.44) * jnp.exp2(log_t * (-LOG2E))
    rq = drift * q
    middle = (PEAK * overdensity * overdensity) * jnp.exp2(log_t * (-1.2 * LOG2E) - drift * rq)
    rq2 = rq + rq
    h2 = jnp.exp2(-2.0 * q)
    steps = [h2 * m for m in masks]
    sides = []
    for ratio in (jnp.exp2(rq2 - q), jnp.exp2(-rq2 - q)):
        term = middle
        side = []
        for j in range(BAND):
            if j:
                ratio = ratio * steps[j - 1]
            term = term * ratio
            side.append(term)
        sides.append(side)
    return sides[1][::-1] + [middle] + sides[0]


def route(terms, displacement):
    zero = jnp.zeros_like(terms[0])
    u = displacement + BAND
    bit0 = (u & 1) != 0
    bit1 = (u & 2) != 0
    low = u < 4
    mid = u < 8

    def shift(values, by, bit):
        size = len(values)
        out = []
        for i in range(size + by):
            here = values[i] if i < size else zero
            there = values[i - by] if i >= by else zero
            out.append(jnp.where(bit, there, here))
        return out

    v = shift(shift(terms, 1, bit0), 2, bit1)
    slots = []
    for i in range(2 * REACH + 1):
        a = v[i] if i < 12 else zero
        b = v[i - 4] if 4 <= i < 16 else zero
        c = v[i - 8] if 8 <= i else zero
        if i < 4:
            slots.append(jnp.where(low, a, zero))
        elif i < 8:
            slots.append(jnp.where(low, a, jnp.where(mid, b, zero)))
        elif i < 12:
            slots.append(jnp.where(low, a, jnp.where(mid, b, c)))
        elif i < 16:
            slots.append(jnp.where(low, zero, jnp.where(mid, b, c)))
        else:
            slots.append(jnp.where(mid, zero, c))
    return slots


def kernel(
    nx, nz,
    width_ref, od_ref, th_ref, dr_ref, dp_ref,
    tau_ref, scale_ref,
    fields, moves, ext, lines, arrived, edge_out, edge_in, row, rows,
    in_sem, edge_ssem, edge_rsem, line_ssem, line_rsem, row_ssem, row_rsem, out_sem,
):
    length, columns, lanes = od_ref.shape
    tiles = columns // 8
    count = nx * nz
    high = nx // tiles
    gx = lax.axis_index("gx")
    gz = lax.axis_index("gz")
    me = gz * nx + gx
    holders = columns // nx
    holds = gz < holders

    def device(index):
        return {"gx": lax.rem(index, nx), "gz": lax.div(index, nx)}

    barrier = pltpu.get_barrier_semaphore()

    def input_copies(t):
        at = pl.ds(pl.multiple_of(t * 8, 8), 8)
        found = [
            pltpu.make_async_copy(ref.at[:, at, :], fields.at[k, t], in_sem.at[k, t])
            for k, ref in enumerate((od_ref, th_ref, dr_ref))
        ]
        return found + [pltpu.make_async_copy(dp_ref.at[:, at, :], moves.at[t], in_sem.at[3, t])]

    @pl.loop(0, tiles)
    def _(t):
        for copy in input_copies(t):
            copy.start()

    @pl.loop(1, count)
    def _(k):
        pl.semaphore_signal(
            barrier, inc=1, device_id=device(lax.rem(me + k, count)),
            device_id_type=pl.DeviceIdType.MESH,
        )

    before = device(lax.rem(me + count - 1, count))
    after = device(lax.rem(me + 1, count))

    def ext_rows(e, t):
        return pl.ds(pl.multiple_of(e * columns + t * 8, 8), 8)

    def deposit(t):
        for copy in input_copies(t):
            copy.wait()
        sublane = lax.broadcasted_iota(jnp.int32, (8, lanes), 0)
        width = jnp.zeros((8, lanes), jnp.int32)
        for s in range(8):
            width = jnp.where(sublane == s, width_ref[t * 8 + s], width)
        masks = [jnp.where(width >= j, 1.0, 0.0).astype(jnp.float32) for j in (2, 3, 4)]
        zero = jnp.zeros((8, lanes), jnp.float32)

        def group(g, window):
            window = list(window)
            for k in range(8):
                z = g * 8 + k
                terms = spread_terms(fields[0, t, z], fields[1, t, z], fields[2, t, z], masks)
                slots = route(terms, moves[t, z])
                window = [w + s for w, s in zip(window, slots)] + slots[len(window):]
                ext[ext_rows(z, t), :] = window[0]
                window = window[1:]
            return tuple(window)

        window = lax.fori_loop(0, length // 8, group, (zero,) * (2 * REACH))
        for k in range(2 * REACH):
            ext[ext_rows(length + k, t), :] = window[k]

    def edge_copies(t):
        return [
            pltpu.make_async_remote_copy(
                src_ref=edge_out.at[k, t], dst_ref=edge_in.at[k, t],
                send_sem=edge_ssem.at[k, t], recv_sem=edge_rsem.at[k, t],
                device_id=target, device_id_type=pl.DeviceIdType.MESH,
            )
            for k, target in enumerate((after, before))
        ]

    def send_edges(t):
        for k in range(REACH):
            edge_out[0, t, k] = ext[ext_rows(length + REACH + k, t), :]
            edge_out[1, t, k] = ext[ext_rows(k, t), :]
        for copy in edge_copies(t):
            copy.start()

    def finish(t):
        for copy in edge_copies(t):
            copy.wait_recv()
        for k in range(REACH):
            ext[ext_rows(REACH + k, t), :] += edge_in[0, t, k]
            ext[ext_rows(length + k, t), :] += edge_in[1, t, k]

        @pl.loop(0, 8)
        def _(step):
            s = lax.rem(step + me, 8)
            column = t * 8 + s
            for z in range(0, length, 8):
                lines[column, z:z + 8, :] = ext[
                    pl.ds((z + REACH) * columns + column, 8, stride=columns), :
                ]
            hz = lax.div(s, high)
            hx = lax.rem(s, high) * tiles + lax.rem(t + (tiles - lax.rem(hz * (tiles // 2), tiles)), tiles)
            holder = hz * nx + hx

            @pl.when(holder == me)
            def _():
                arrived[me] = lines[column]

            @pl.when(holder != me)
            def _():
                pltpu.make_async_remote_copy(
                    src_ref=lines.at[column], dst_ref=arrived.at[me],
                    send_sem=line_ssem, recv_sem=line_rsem,
                    device_id={"gx": hx, "gz": hz}, device_id_type=pl.DeviceIdType.MESH,
                ).start()

    deposit(0)
    pl.semaphore_wait(barrier, count - 1)
    send_edges(0)

    @pl.loop(1, tiles)
    def _(t):
        deposit(t)
        send_edges(t)
        finish(t - 1)

    finish(tiles - 1)

    tau_copy = pltpu.make_async_copy(
        ext.at[pl.ds(REACH * columns, length * columns), :], tau_ref, out_sem
    )
    tau_copy.start()

    my_column = lax.rem(gx + lax.rem(gz * (tiles // 2), tiles), tiles) * 8 + lax.div(gx, tiles) + high * gz

    def row_copy(target):
        return pltpu.make_async_remote_copy(
            src_ref=row.at[0], dst_ref=rows.at[my_column],
            send_sem=row_ssem, recv_sem=row_rsem,
            device_id=target, device_id_type=pl.DeviceIdType.MESH,
        )

    def wait_bytes(ref, sem):
        pltpu.make_async_copy(ref, ref, sem).wait()

    @pl.when(holds)
    def _():
        wait_bytes(arrived.at[pl.ds(0, count - 1)], line_rsem)
        cells = float(count * length)

        def newton(_, level):
            factor = jnp.exp(level)
            m = jnp.broadcast_to(factor * (-LOG2E), (8, lanes))
            zero = jnp.zeros((8, lanes), jnp.float32)

            def block(i, sums):
                first, second = list(sums[:4]), list(sums[4:])
                for k in range(length // 8):
                    tau = arrived[i, 8 * k:8 * k + 8, :]
                    damped = jnp.exp2(m * tau)
                    first[k % 4] += damped
                    second[k % 4] += tau * damped
                return tuple(first + second)

            sums = lax.fori_loop(0, count, block, (zero,) * 8, unroll=4)
            first = jnp.sum((sums[0] + sums[1]) + (sums[2] + sums[3]), axis=0, keepdims=True)
            second = jnp.sum((sums[4] + sums[5]) + (sums[6] + sums[7]), axis=0, keepdims=True)
            return level - 0.4 * (first / cells - 0.35) / (-factor * second / cells)

        level = lax.fori_loop(0, ITERS, newton, jnp.zeros((1, lanes), jnp.float32))
        row[0] = jnp.exp(level)
        rows[my_column] = row[0]

        @pl.loop(1, count)
        def _(k):
            row_copy(device(lax.rem(me + k, count))).start()

        wait_bytes(rows.at[pl.ds(0, columns - 1)], row_rsem)
        wait_bytes(lines.at[pl.ds(0, columns - 1)], line_ssem)

        @pl.loop(1, count)
        def _(k):
            wait_bytes(row.at[0], row_ssem)

    @pl.when(jnp.logical_not(holds))
    def _():
        wait_bytes(rows, row_rsem)
        wait_bytes(lines, line_ssem)

    for x in range(columns):
        scale_ref[x:x + 1, :] = rows[x]

    @pl.loop(0, tiles)
    def _(t):
        for copy in edge_copies(t):
            copy.wait_send()

    tau_copy.wait()


def shards(nx, nz, overdensity_ratio, thermal_state, residual_drift, peculiar_displacement, doppler_spread):
    _, length, columns, lanes = overdensity_ratio.shape
    tiles = columns // 8
    count = nx * nz
    assert columns % 8 == 0 and nx % tiles == 0 and columns % nx == 0 and columns // nx <= nz
    assert length % 8 == 0 and length >= 2 * REACH
    f32 = jnp.float32
    scratch = [
        pltpu.VMEM((3, tiles, length, 8, lanes), f32),
        pltpu.VMEM((tiles, length, 8, lanes), jnp.int32),
        pltpu.VMEM(((length + 2 * REACH) * columns, lanes), f32),
        pltpu.VMEM((columns, length, lanes), f32),
        pltpu.VMEM((count, length, lanes), f32),
        pltpu.VMEM((2, tiles, REACH, 8, lanes), f32),
        pltpu.VMEM((2, tiles, REACH, 8, lanes), f32),
        pltpu.VMEM((1, 1, lanes), f32),
        pltpu.VMEM((columns, 1, lanes), f32),
        pltpu.SemaphoreType.DMA((4, tiles)),
        pltpu.SemaphoreType.DMA((2, tiles)),
        pltpu.SemaphoreType.DMA((2, tiles)),
    ] + [pltpu.SemaphoreType.DMA(())] * 5
    used = 4 * lanes * (columns * length * 6 + 2 * REACH * columns * 4 + count * length)
    tau, scale = pl.pallas_call(
        functools.partial(kernel, nx, nz),
        out_shape=(
            jax.ShapeDtypeStruct((length * columns, lanes), f32),
            jax.ShapeDtypeStruct((columns, lanes), f32),
        ),
        in_specs=[pl.BlockSpec(memory_space=pltpu.SMEM)] + [pl.BlockSpec(memory_space=pl.ANY)] * 4,
        out_specs=(pl.BlockSpec(memory_space=pl.ANY), pl.BlockSpec(memory_space=pltpu.VMEM)),
        scratch_shapes=scratch,
        compiler_params=pltpu.CompilerParams(
            collective_id=0, has_side_effects=True, vmem_limit_bytes=used + (4 << 20)
        ),
        name="forest",
    )(doppler_spread, overdensity_ratio[0], thermal_state[0], residual_drift[0], peculiar_displacement[0])
    flux = jnp.exp(-scale[None] * tau.reshape(length, columns, lanes))
    share = columns // nx
    return flux[None], lax.dynamic_slice_in_dim(scale, lax.axis_index("gx") * share, share, 0)


def solution(mesh):
    placed = (
        P("gz", "gx", None, None),
        P("gz", "gx", None, None),
        P("gz", "gx", None, None),
        P("gz", "gx", None, None),
        P(),
    )
    return jax.shard_map(
        functools.partial(shards, mesh.shape["gx"], mesh.shape["gz"]),
        mesh=mesh,
        in_specs=placed,
        out_specs=(P("gz", "gx", None, None), P("gx", None)),
        check_vma=False,
    )
```

```python
import functools
import math

import jax
import jax.numpy as jnp
from jax import lax
from jax.experimental import pallas as pl
from jax.experimental.pallas import tpu as pltpu
from jax.sharding import PartitionSpec as P

ITERS = 8
REACH = 8
BAND = 4
LOG2E = math.log2(math.e)
PEAK = 0.05 / (1.2 * math.sqrt(math.pi))


def spread_terms(overdensity, thermal, drift, masks):
    log_t = jnp.log(thermal)
    q = (LOG2E / 1.44) * jnp.exp2(log_t * (-LOG2E))
    rq = drift * q
    middle = (PEAK * overdensity * overdensity) * jnp.exp2(log_t * (-1.2 * LOG2E) - drift * rq)
    rq2 = rq + rq
    h2 = jnp.exp2(-2.0 * q)
    steps = [h2 * m for m in masks]
    sides = []
    for ratio in (jnp.exp2(rq2 - q), jnp.exp2(-rq2 - q)):
        term = middle
        side = []
        for j in range(BAND):
            if j:
                ratio = ratio * steps[j - 1]
            term = term * ratio
            side.append(term)
        sides.append(side)
    return sides[1][::-1] + [middle] + sides[0]


def route(terms, displacement):
    zero = jnp.zeros_like(terms[0])
    u = displacement + BAND
    bit0 = (u & 1) != 0
    bit1 = (u & 2) != 0
    low = u < 4
    mid = u < 8

    def shift(values, by, bit):
        size = len(values)
        out = []
        for i in range(size + by):
            here = values[i] if i < size else zero
            there = values[i - by] if i >= by else zero
            out.append(jnp.where(bit, there, here))
        return out

    v = shift(shift(terms, 1, bit0), 2, bit1)
    slots = []
    for i in range(2 * REACH + 1):
        a = v[i] if i < 12 else zero
        b = v[i - 4] if 4 <= i < 16 else zero
        c = v[i - 8] if 8 <= i else zero
        if i < 4:
            slots.append(jnp.where(low, a, zero))
        elif i < 8:
            slots.append(jnp.where(low, a, jnp.where(mid, b, zero)))
        elif i < 12:
            slots.append(jnp.where(low, a, jnp.where(mid, b, c)))
        elif i < 16:
            slots.append(jnp.where(low, zero, jnp.where(mid, b, c)))
        else:
            slots.append(jnp.where(mid, zero, c))
    return slots


def kernel(
    nx, nz,
    spread_ref, od_ref, th_ref, dr_ref, dp_ref,
    tau_ref, scale_ref,
    width_ref, fields, moves, ext, lines, arrived, edge_out, edge_in, row, rows,
    in_sem, edge_ssem, edge_rsem, line_ssem, line_rsem, row_ssem, row_rsem, out_sem, width_sem,
):
    length, columns, lanes = od_ref.shape
    tiles = columns // 8
    count = nx * nz
    high = nx // tiles
    gx = lax.axis_index("gx")
    gz = lax.axis_index("gz")
    me = gz * nx + gx
    holders = columns // nx
    holds = gz < holders

    def device(index):
        return {"gx": lax.rem(index, nx), "gz": lax.div(index, nx)}

    def wrap(index, size):
        return jnp.where(index >= size, index - size, index)

    barrier = pltpu.get_barrier_semaphore()

    def input_copies(t):
        at = pl.ds(pl.multiple_of(t * 8, 8), 8)
        found = [
            pltpu.make_async_copy(ref.at[:, at, :], fields.at[k, t], in_sem.at[k, t])
            for k, ref in enumerate((od_ref, th_ref, dr_ref))
        ]
        return found + [pltpu.make_async_copy(dp_ref.at[:, at, :], moves.at[t], in_sem.at[3, t])]

    width_copy = pltpu.make_async_copy(spread_ref, width_ref, width_sem)
    width_copy.start()

    @pl.loop(0, tiles)
    def _(t):
        for copy in input_copies(t):
            copy.start()

    @pl.loop(1, count)
    def _(k):
        pl.semaphore_signal(
            barrier, inc=1, device_id=device(lax.rem(me + k, count)),
            device_id_type=pl.DeviceIdType.MESH,
        )

    before = device(lax.rem(me + count - 1, count))
    after = device(lax.rem(me + 1, count))

    def ext_rows(e, t):
        return pl.ds(pl.multiple_of(e * columns + t * 8, 8), 8)

    def deposit(t):
        for copy in input_copies(t):
            copy.wait()
        sublane = lax.broadcasted_iota(jnp.int32, (8, lanes), 0)
        width = jnp.zeros((8, lanes), jnp.int32)
        for s in range(8):
            width = jnp.where(sublane == s, width_ref[t * 8 + s], width)
        masks = [jnp.where(width >= j, 1.0, 0.0).astype(jnp.float32) for j in (2, 3, 4)]
        zero = jnp.zeros((8, lanes), jnp.float32)

        def group(g, window):
            window = list(window)
            for k in range(8):
                z = g * 8 + k
                terms = spread_terms(fields[0, t, z], fields[1, t, z], fields[2, t, z], masks)
                slots = route(terms, moves[t, z])
                window = [w + s for w, s in zip(window, slots)] + slots[len(window):]
                ext[ext_rows(z, t), :] = window[0]
                window = window[1:]
            return tuple(window)

        window = lax.fori_loop(0, length // 8, group, (zero,) * (2 * REACH))
        for k in range(2 * REACH):
            ext[ext_rows(length + k, t), :] = window[k]

    def edge_copies(t):
        return [
            pltpu.make_async_remote_copy(
                src_ref=edge_out.at[k, t], dst_ref=edge_in.at[k, t],
                send_sem=edge_ssem.at[k, t], recv_sem=edge_rsem.at[k, t],
                device_id=target, device_id_type=pl.DeviceIdType.MESH,
            )
            for k, target in enumerate((after, before))
        ]

    def send_edges(t):
        for k in range(REACH):
            edge_out[0, t, k] = ext[ext_rows(length + REACH + k, t), :]
            edge_out[1, t, k] = ext[ext_rows(k, t), :]
        for copy in edge_copies(t):
            copy.start()

    def finish(t):
        for copy in edge_copies(t):
            copy.wait_recv()
        for k in range(REACH):
            ext[ext_rows(REACH + k, t), :] += edge_in[0, t, k]
            ext[ext_rows(length + k, t), :] += edge_in[1, t, k]

        @pl.loop(0, 8)
        def _(step):
            s = lax.rem(step + me, 8)
            column = t * 8 + s
            for z in range(0, length, 8):
                lines[column, z:z + 8, :] = ext[
                    pl.ds((z + REACH) * columns + column, 8, stride=columns), :
                ]
            hz = lax.div(s, high)
            hx = lax.rem(s, high) * tiles + lax.rem(t + (tiles - lax.rem(hz * (tiles // 2), tiles)), tiles)
            holder = hz * nx + hx

            @pl.when(holder == me)
            def _():
                arrived[me] = lines[column]

            @pl.when(holder != me)
            def _():
                pltpu.make_async_remote_copy(
                    src_ref=lines.at[column], dst_ref=arrived.at[me],
                    send_sem=line_ssem, recv_sem=line_rsem,
                    device_id={"gx": hx, "gz": hz}, device_id_type=pl.DeviceIdType.MESH,
                ).start()

    width_copy.wait()
    deposit(0)
    pl.semaphore_wait(barrier, count - 1)
    send_edges(0)

    @pl.loop(1, tiles)
    def _(t):
        deposit(t)
        send_edges(t)
        finish(t - 1)

    finish(tiles - 1)

    tau_copy = pltpu.make_async_copy(
        ext.at[pl.ds(REACH * columns, length * columns), :], tau_ref, out_sem
    )
    tau_copy.start()

    my_column = lax.rem(gx + lax.rem(gz * (tiles // 2), tiles), tiles) * 8 + lax.div(gx, tiles) + high * gz

    def row_copy(target):
        return pltpu.make_async_remote_copy(
            src_ref=row.at[0], dst_ref=rows.at[my_column],
            send_sem=row_ssem, recv_sem=row_rsem,
            device_id=target, device_id_type=pl.DeviceIdType.MESH,
        )

    def wait_bytes(ref, sem):
        pltpu.make_async_copy(ref, ref, sem).wait()

    @pl.when(holds)
    def _():
        wait_bytes(arrived.at[pl.ds(0, count - 1)], line_rsem)
        cells = float(count * length)

        def newton(_, level):
            factor = jnp.exp(level)
            m = jnp.broadcast_to(factor * (-LOG2E), (8, lanes))
            zero = jnp.zeros((8, lanes), jnp.float32)

            def block(i, sums):
                first, second = list(sums[:4]), list(sums[4:])
                for k in range(length // 8):
                    tau = arrived[i, 8 * k:8 * k + 8, :]
                    damped = jnp.exp2(m * tau)
                    first[k % 4] += damped
                    second[k % 4] += tau * damped
                return tuple(first + second)

            sums = lax.fori_loop(0, count, block, (zero,) * 8, unroll=4)
            first = jnp.sum((sums[0] + sums[1]) + (sums[2] + sums[3]), axis=0, keepdims=True)
            second = jnp.sum((sums[4] + sums[5]) + (sums[6] + sums[7]), axis=0, keepdims=True)
            return level - 0.4 * (first / cells - 0.35) / (-factor * second / cells)

        level = lax.fori_loop(0, ITERS, newton, jnp.zeros((1, lanes), jnp.float32))
        row[0] = jnp.exp(level)
        rows[my_column] = row[0]

        for b in range(nz):
            @pl.loop(0 if b else 1, nx)
            def _(a, b=b):
                row_copy({"gx": wrap(gx + a, nx), "gz": wrap(gz + b, nz)}).start()

        wait_bytes(rows.at[pl.ds(0, columns - 1)], row_rsem)
        wait_bytes(lines.at[pl.ds(0, columns - 1)], line_ssem)

        blocks, rest = divmod(count - 1, length)
        if blocks:
            wait_bytes(arrived.at[pl.ds(0, blocks)], row_ssem)
        if rest:
            wait_bytes(arrived.at[0, pl.ds(0, rest)], row_ssem)

    @pl.when(jnp.logical_not(holds))
    def _():
        wait_bytes(rows, row_rsem)
        wait_bytes(lines, line_ssem)

    for x in range(columns):
        scale_ref[x:x + 1, :] = rows[x]

    @pl.loop(0, tiles)
    def _(t):
        for copy in edge_copies(t):
            copy.wait_send()

    tau_copy.wait()


def shards(nx, nz, overdensity_ratio, thermal_state, residual_drift, peculiar_displacement, doppler_spread):
    _, length, columns, lanes = overdensity_ratio.shape
    tiles = columns // 8
    count = nx * nz
    assert columns % 8 == 0 and nx % tiles == 0 and columns % nx == 0 and columns // nx <= nz
    assert length % 8 == 0 and length >= 2 * REACH
    f32 = jnp.float32
    scratch = [
        pltpu.SMEM((columns,), jnp.int32),
        pltpu.VMEM((3, tiles, length, 8, lanes), f32),
        pltpu.VMEM((tiles, length, 8, lanes), jnp.int32),
        pltpu.VMEM(((length + 2 * REACH) * columns, lanes), f32),
        pltpu.VMEM((columns, length, lanes), f32),
        pltpu.VMEM((count, length, lanes), f32),
        pltpu.VMEM((2, tiles, REACH, 8, lanes), f32),
        pltpu.VMEM((2, tiles, REACH, 8, lanes), f32),
        pltpu.VMEM((1, 1, lanes), f32),
        pltpu.VMEM((columns, 1, lanes), f32),
        pltpu.SemaphoreType.DMA((4, tiles)),
        pltpu.SemaphoreType.DMA((2, tiles)),
        pltpu.SemaphoreType.DMA((2, tiles)),
    ] + [pltpu.SemaphoreType.DMA(())] * 6
    used = 4 * lanes * (columns * length * 6 + 2 * REACH * columns * 4 + count * length)
    bricks = [
        pltpu.with_memory_space_constraint(value[0], pltpu.HBM)
        for value in (overdensity_ratio, thermal_state, residual_drift, peculiar_displacement)
    ]
    tau, scale = pl.pallas_call(
        functools.partial(kernel, nx, nz),
        out_shape=(
            jax.ShapeDtypeStruct((length * columns, lanes), f32),
            jax.ShapeDtypeStruct((columns, lanes), f32),
        ),
        in_specs=[pl.BlockSpec(memory_space=pltpu.HBM)] * 5,
        out_specs=(pl.BlockSpec(memory_space=pl.ANY), pl.BlockSpec(memory_space=pltpu.VMEM)),
        scratch_shapes=scratch,
        compiler_params=pltpu.CompilerParams(
            collective_id=0, has_side_effects=True, vmem_limit_bytes=used + (4 << 20)
        ),
        name="forest",
    )(pltpu.with_memory_space_constraint(doppler_spread, pltpu.HBM), *bricks)
    flux = jnp.exp(-scale[None] * tau.reshape(length, columns, lanes))
    share = columns // nx
    return flux[None], lax.dynamic_slice_in_dim(scale, lax.axis_index("gx") * share, share, 0)


def solution(mesh):
    placed = (
        P("gz", "gx", None, None),
        P("gz", "gx", None, None),
        P("gz", "gx", None, None),
        P("gz", "gx", None, None),
        P(),
    )
    return jax.shard_map(
        functools.partial(shards, mesh.shape["gx"], mesh.shape["gz"]),
        mesh=mesh,
        in_specs=placed,
        out_specs=(P("gz", "gx", None, None), P("gx", None)),
        check_vma=False,
    )
```

```python
import functools
import math

import jax
import jax.numpy as jnp
from jax import lax
from jax.experimental import pallas as pl
from jax.experimental.pallas import tpu as pltpu
from jax.sharding import PartitionSpec as P

ITERS = 8
REACH = 8
BAND = 4
LOG2E = math.log2(math.e)
PEAK = 0.05 / (1.2 * math.sqrt(math.pi))


def spread_terms(overdensity, thermal, drift, masks):
    log_t = jnp.log(thermal)
    q = (LOG2E / 1.44) * jnp.exp2(log_t * (-LOG2E))
    rq = drift * q
    middle = (PEAK * overdensity * overdensity) * jnp.exp2(log_t * (-1.2 * LOG2E) - drift * rq)
    rq2 = rq + rq
    h2 = jnp.exp2(-2.0 * q)
    steps = [h2 * m for m in masks]
    sides = []
    for ratio in (jnp.exp2(rq2 - q), jnp.exp2(-rq2 - q)):
        term = middle
        side = []
        for j in range(BAND):
            if j:
                ratio = ratio * steps[j - 1]
            term = term * ratio
            side.append(term)
        sides.append(side)
    return sides[1][::-1] + [middle] + sides[0]


def route(terms, displacement):
    zero = jnp.zeros_like(terms[0])
    u = displacement + BAND
    bit0 = (u & 1) != 0
    bit1 = (u & 2) != 0
    low = u < 4
    mid = u < 8

    def shift(values, by, bit):
        size = len(values)
        out = []
        for i in range(size + by):
            here = values[i] if i < size else zero
            there = values[i - by] if i >= by else zero
            out.append(jnp.where(bit, there, here))
        return out

    v = shift(shift(terms, 1, bit0), 2, bit1)
    slots = []
    for i in range(2 * REACH + 1):
        a = v[i] if i < 12 else zero
        b = v[i - 4] if 4 <= i < 16 else zero
        c = v[i - 8] if 8 <= i else zero
        if i < 4:
            slots.append(jnp.where(low, a, zero))
        elif i < 8:
            slots.append(jnp.where(low, a, jnp.where(mid, b, zero)))
        elif i < 12:
            slots.append(jnp.where(low, a, jnp.where(mid, b, c)))
        elif i < 16:
            slots.append(jnp.where(low, zero, jnp.where(mid, b, c)))
        else:
            slots.append(jnp.where(mid, zero, c))
    return slots


def kernel(
    nx, nz,
    spread_ref, od_ref, th_ref, dr_ref, dp_ref,
    tau_ref, scale_ref,
    width_ref, fields, moves, ext, lines, arrived, edge_out, edge_in, row, rows,
    in_sem, edge_ssem, edge_rsem, line_ssem, line_rsem, row_ssem, row_rsem, out_sem, width_sem,
):
    length, columns, lanes = od_ref.shape
    tiles = columns // 8
    count = nx * nz
    high = nx // tiles
    gx = lax.axis_index("gx")
    gz = lax.axis_index("gz")
    me = gz * nx + gx
    holders = columns // nx
    holds = gz < holders

    def device(index):
        return {"gx": lax.rem(index, nx), "gz": lax.div(index, nx)}

    def wrap(index, size):
        return jnp.where(index >= size, index - size, index)

    barrier = pltpu.get_barrier_semaphore()
    for b in range(nz):
        @pl.loop(0 if b else 1, nx)
        def _(a, b=b):
            pl.semaphore_signal(
                barrier, inc=1,
                device_id={"gx": wrap(gx + a, nx), "gz": wrap(gz + b, nz)},
                device_id_type=pl.DeviceIdType.MESH,
            )

    def input_copies(t):
        at = pl.ds(pl.multiple_of(t * 8, 8), 8)
        found = [
            pltpu.make_async_copy(ref.at[:, at, :], fields.at[k, t], in_sem.at[k, t])
            for k, ref in enumerate((od_ref, th_ref, dr_ref))
        ]
        return found + [pltpu.make_async_copy(dp_ref.at[:, at, :], moves.at[t], in_sem.at[3, t])]

    width_copy = pltpu.make_async_copy(spread_ref, width_ref, width_sem)
    width_copy.start()

    @pl.loop(0, tiles)
    def _(t):
        for copy in input_copies(t):
            copy.start()

    before = device(lax.rem(me + count - 1, count))
    after = device(lax.rem(me + 1, count))

    def ext_rows(e, t):
        return pl.ds(pl.multiple_of(e * columns + t * 8, 8), 8)

    def tile_masks(t):
        sublane = lax.broadcasted_iota(jnp.int32, (8, lanes), 0)
        width = jnp.zeros((8, lanes), jnp.int32)
        for s in range(8):
            width = jnp.where(sublane == s, width_ref[t * 8 + s], width)
        return [jnp.where(width >= j, 1.0, 0.0).astype(jnp.float32) for j in (2, 3, 4)]

    empty = (jnp.zeros((8, lanes), jnp.float32),) * (2 * REACH)

    def group(t, masks, g, window):
        done = []
        for k in range(8):
            z = g * 8 + k
            terms = spread_terms(fields[0, t, z], fields[1, t, z], fields[2, t, z], masks)
            slots = route(terms, moves[t, z])
            window = [w + s for w, s in zip(window, slots)] + slots[len(window):]
            done.append(window[0])
            window = window[1:]
        return done, tuple(window)

    def deposit(t):
        masks = tile_masks(t)

        def body(g, window):
            done, window = group(t, masks, g, window)
            for k in range(8):
                ext[ext_rows(g * 8 + k, t), :] = done[k]
            return window

        window = lax.fori_loop(0, length // 8, body, empty)
        for k in range(2 * REACH):
            ext[ext_rows(length + k, t), :] = window[k]

    def wait_inputs(t):
        for copy in input_copies(t):
            copy.wait()

    def early_edges(t):
        masks = tile_masks(t)

        @pl.loop(0, 2)
        def _(side):
            low = side == 1
            done, window = group(t, masks, jnp.where(low, 0, length // 8 - 1), empty)
            for k in range(REACH):
                edge_out[side, t, k] = jnp.where(low, done[k], window[REACH + k])

    def edge_copies(t):
        return [
            pltpu.make_async_remote_copy(
                src_ref=edge_out.at[k, t], dst_ref=edge_in.at[k, t],
                send_sem=edge_ssem.at[k, t], recv_sem=edge_rsem.at[k, t],
                device_id=target, device_id_type=pl.DeviceIdType.MESH,
            )
            for k, target in enumerate((after, before))
        ]

    def send_edges(t):
        for copy in edge_copies(t):
            copy.start()

    def finish(t):
        for copy in edge_copies(t):
            copy.wait_recv()
        for k in range(REACH):
            ext[ext_rows(REACH + k, t), :] += edge_in[0, t, k]
            ext[ext_rows(length + k, t), :] += edge_in[1, t, k]

        @pl.loop(0, 8)
        def _(step):
            s = lax.rem(step + me, 8)
            column = t * 8 + s
            for z in range(0, length, 8):
                lines[column, z:z + 8, :] = ext[
                    pl.ds((z + REACH) * columns + column, 8, stride=columns), :
                ]
            hz = lax.div(s, high)
            hx = lax.rem(s, high) * tiles + lax.rem(t + (tiles - lax.rem(hz * (tiles // 2), tiles)), tiles)
            holder = hz * nx + hx

            @pl.when(holder == me)
            def _():
                arrived[me] = lines[column]

            @pl.when(holder != me)
            def _():
                pltpu.make_async_remote_copy(
                    src_ref=lines.at[column], dst_ref=arrived.at[me],
                    send_sem=line_ssem, recv_sem=line_rsem,
                    device_id={"gx": hx, "gz": hz}, device_id_type=pl.DeviceIdType.MESH,
                ).start()

    width_copy.wait()
    @pl.loop(0, tiles)
    def _(t):
        wait_inputs(t)
        early_edges(t)

    pl.semaphore_wait(barrier, count - 1)

    @pl.loop(0, tiles)
    def _(t):
        send_edges(t)

    @pl.loop(0, tiles)
    def _(t):
        deposit(t)
        finish(t)

    tau_copy = pltpu.make_async_copy(
        ext.at[pl.ds(REACH * columns, length * columns), :], tau_ref, out_sem
    )
    tau_copy.start()

    my_column = lax.rem(gx + lax.rem(gz * (tiles // 2), tiles), tiles) * 8 + lax.div(gx, tiles) + high * gz

    def row_copy(target):
        return pltpu.make_async_remote_copy(
            src_ref=row.at[0], dst_ref=rows.at[my_column],
            send_sem=row_ssem, recv_sem=row_rsem,
            device_id=target, device_id_type=pl.DeviceIdType.MESH,
        )

    def wait_bytes(ref, sem):
        pltpu.make_async_copy(ref, ref, sem).wait()

    @pl.when(holds)
    def _():
        wait_bytes(arrived.at[pl.ds(0, count - 1)], line_rsem)
        cells = float(count * length)

        def newton(_, level):
            factor = jnp.exp(level)
            m = jnp.broadcast_to(factor * (-LOG2E), (8, lanes))
            zero = jnp.zeros((8, lanes), jnp.float32)

            def block(i, sums):
                first, second = list(sums[:4]), list(sums[4:])
                for k in range(length // 8):
                    tau = arrived[i, 8 * k:8 * k + 8, :]
                    damped = jnp.exp2(m * tau)
                    first[k % 4] += damped
                    second[k % 4] += tau * damped
                return tuple(first + second)

            sums = lax.fori_loop(0, count, block, (zero,) * 8, unroll=4)
            first = jnp.sum((sums[0] + sums[1]) + (sums[2] + sums[3]), axis=0, keepdims=True)
            second = jnp.sum((sums[4] + sums[5]) + (sums[6] + sums[7]), axis=0, keepdims=True)
            return level - 0.4 * (first / cells - 0.35) / (-factor * second / cells)

        level = lax.fori_loop(0, ITERS, newton, jnp.zeros((1, lanes), jnp.float32))
        row[0] = jnp.exp(level)
        rows[my_column] = row[0]

        for b in range(nz):
            @pl.loop(0 if b else 1, nx)
            def _(a, b=b):
                row_copy({"gx": wrap(gx + a, nx), "gz": wrap(gz + b, nz)}).start()

        wait_bytes(rows.at[pl.ds(0, columns - 1)], row_rsem)
        wait_bytes(lines.at[pl.ds(0, columns - 1)], line_ssem)

        blocks, rest = divmod(count - 1, length)
        if blocks:
            wait_bytes(arrived.at[pl.ds(0, blocks)], row_ssem)
        if rest:
            wait_bytes(arrived.at[0, pl.ds(0, rest)], row_ssem)

    @pl.when(jnp.logical_not(holds))
    def _():
        wait_bytes(rows, row_rsem)
        wait_bytes(lines, line_ssem)

    for x in range(columns):
        scale_ref[x:x + 1, :] = rows[x]

    @pl.loop(0, tiles)
    def _(t):
        for copy in edge_copies(t):
            copy.wait_send()

    tau_copy.wait()


def shards(nx, nz, overdensity_ratio, thermal_state, residual_drift, peculiar_displacement, doppler_spread):
    _, length, columns, lanes = overdensity_ratio.shape
    tiles = columns // 8
    count = nx * nz
    assert columns % 8 == 0 and nx % tiles == 0 and columns % nx == 0 and columns // nx <= nz
    assert length % 8 == 0 and length >= 2 * REACH
    f32 = jnp.float32
    scratch = [
        pltpu.SMEM((columns,), jnp.int32),
        pltpu.VMEM((3, tiles, length, 8, lanes), f32),
        pltpu.VMEM((tiles, length, 8, lanes), jnp.int32),
        pltpu.VMEM(((length + 2 * REACH) * columns, lanes), f32),
        pltpu.VMEM((columns, length, lanes), f32),
        pltpu.VMEM((count, length, lanes), f32),
        pltpu.VMEM((2, tiles, REACH, 8, lanes), f32),
        pltpu.VMEM((2, tiles, REACH, 8, lanes), f32),
        pltpu.VMEM((1, 1, lanes), f32),
        pltpu.VMEM((columns, 1, lanes), f32),
        pltpu.SemaphoreType.DMA((4, tiles)),
        pltpu.SemaphoreType.DMA((2, tiles)),
        pltpu.SemaphoreType.DMA((2, tiles)),
    ] + [pltpu.SemaphoreType.DMA(())] * 6
    used = 4 * lanes * (columns * length * 6 + 2 * REACH * columns * 4 + count * length)
    bricks = [
        pltpu.with_memory_space_constraint(value[0], pltpu.HBM)
        for value in (overdensity_ratio, thermal_state, residual_drift, peculiar_displacement)
    ]
    tau, scale = pl.pallas_call(
        functools.partial(kernel, nx, nz),
        out_shape=(
            jax.ShapeDtypeStruct((length * columns, lanes), f32),
            jax.ShapeDtypeStruct((columns, lanes), f32),
        ),
        in_specs=[pl.BlockSpec(memory_space=pltpu.HBM)] * 5,
        out_specs=(pl.BlockSpec(memory_space=pl.ANY), pl.BlockSpec(memory_space=pltpu.VMEM)),
        scratch_shapes=scratch,
        compiler_params=pltpu.CompilerParams(
            collective_id=0, has_side_effects=True, vmem_limit_bytes=used + (4 << 20)
        ),
        name="forest",
    )(pltpu.with_memory_space_constraint(doppler_spread, pltpu.HBM), *bricks)
    flux = jnp.exp(-scale[None] * tau.reshape(length, columns, lanes))
    share = columns // nx
    return flux[None], lax.dynamic_slice_in_dim(scale, lax.axis_index("gx") * share, share, 0)


def solution(mesh):
    placed = (
        P("gz", "gx", None, None),
        P("gz", "gx", None, None),
        P("gz", "gx", None, None),
        P("gz", "gx", None, None),
        P(),
    )
    return jax.shard_map(
        functools.partial(shards, mesh.shape["gx"], mesh.shape["gz"]),
        mesh=mesh,
        in_specs=placed,
        out_specs=(P("gz", "gx", None, None), P("gx", None)),
        check_vma=False,
    )
```
